32 devices in a mesh: dp: 4 (over z), expert: 2 (over x), tensor: 4 (over y, core).
Axes of the slice: x: 2, y: 2, z: 4, core: 2. Of those that a mesh axis runs over, the one named last changes fastest.
Arguments:
- tokens: bfloat16 [128, 4096], P(('dp', 'expert', 'tensor')), may hold values from -6 to 6
- routes: int32 [128, 2], P(('dp', 'expert', 'tensor')), may hold values from 0 to 7, all different within a row; in each aligned block of 4 rows (0 to 3, 4 to 7, ...) at most 2 rows name the same one
- gates: float32 [128, 2], P(('dp', 'expert', 'tensor')), may hold values from 0.1 to 1
- d_out: bfloat16 [128, 4096], P(('dp', 'expert', 'tensor')), may hold values from -3 to 3
- w_in: bfloat16 [8, 2, 7168, 4096], P('expert', None, ('dp', 'tensor')), may hold values from -0.09375 to 0.09375
- w_out: bfloat16 [8, 7168, 4096], P('expert', ('dp', 'tensor')), may hold values from -0.0625 to 0.0625
Outputs:
- mixed: bfloat16 [128, 4096], P(('dp', 'expert', 'tensor'))
- d_tokens: bfloat16 [128, 4096], P(('dp', 'expert', 'tensor'))
- d_gates: float32 [128, 2], P(('dp', 'expert', 'tensor'))
- grad_in: bfloat16 [8, 2, 7168, 4096], P('expert', None, ('dp', 'tensor'))
- grad_out: bfloat16 [8, 7168, 4096], P('expert', ('dp', 'tensor'))
The draws below stay inside these ranges and needn't reach their ends.
Inputs may be any that keep to these rules, and one draw needn't show every extreme that they name: `routes`: each token names 2 different experts; among the 4 tokens of one device no expert is named more than 2 times, a bound that some block reaches.
All inputs are finite; a program needn't handle non-finite values.
Results may differ from the reference program's by a relative error of at most 0.0065.
Values may be sent and summed in bfloat16 or wider, within the bound.
No kernel may reach another device: no remote copies, remote signals or barrier semaphores. Data moves between devices by JAX's collectives and lax.ppermute only.
A program may use at most 192 MiB of HBM per device.

```python
import math
import jax
import jax.numpy as jnp
import numpy as np
from jax import lax

D = 4096
FF = 7168
EXPERTS = 8
TOP = 2
TOK_DEV = 4
TOKENS = 128
CAP = 2
N_DP = 4
N_EXPERT = 2
N_TENSOR = 4


def levels(rng, shape, shards, smallest, high):
    loudness = 1.0
    for dim, blocks in shards:
        steps = jax.random.uniform(jax.random.fold_in(jax.random.fold_in(rng, 6), dim), (blocks,), jnp.float32, smallest / len(shards), high / len(shards))
        loudness = loudness * jnp.repeat(jnp.exp(steps), shape[dim] // blocks).reshape((-1,) + (1,) * (len(shape) - 1 - dim))
    return loudness


def routed_block(rng, own, number, rows, number_of, top, bound, skew):
    order = jax.random.permutation(rng, number_of)
    crowded, common = portions_of(number_of, rows * top, bound, skew, True), portions_of(number_of, rows * top, bound, skew, False)
    places = jnp.arange(number_of)

    def named(tallies, offset_by):
        used = int((tallies > 0).sum())
        fixed = max(1, used // 4)
        moved = fixed + (places - fixed + offset_by * (used - fixed)) % max(1, number_of - fixed)
        return jnp.zeros((number_of,), jnp.int32).at[order[jnp.where(places < fixed, places, moved)]].set(jnp.asarray(tallies, jnp.int32))

    tallies = jnp.where(number % 4 == 0, named(crowded, number // 4), named(common, number - number // 4 - 1))
    mixed = jax.random.permutation(jax.random.fold_in(own, 3), number_of)
    source_of, receiver = mixed[0:number_of // 2 * 2:2], mixed[1:number_of // 2 * 2:2]
    slack = jnp.minimum(tallies[source_of] - 1, bound - tallies[receiver]) // 2
    slack = jnp.where((source_of == order[0]) | (receiver == order[0]) | (tallies[receiver] == 0), 0, jnp.maximum(slack, 0))
    moved = jax.random.randint(jax.random.fold_in(own, 4), (number_of // 2,), 0, 1 << 20) % (slack + 1)
    tallies = tallies.at[source_of].add(-moved).at[receiver].add(moved)
    labels = jnp.searchsorted(jnp.cumsum(tallies), jnp.arange(rows * top), side="right").astype(jnp.int32)
    table = labels.reshape(top, rows).T
    table = table[jax.random.permutation(jax.random.fold_in(own, 1), rows)]
    offset_by = jax.random.randint(jax.random.fold_in(own, 2), (rows, 1), 0, top)
    return jnp.take_along_axis(table, (jnp.arange(top)[None, :] + offset_by) % top, axis=1)


def portions_of(amount, total, most, slope, full):
    weights = [(1 << 20) // math.isqrt(rank ** slope) + 1 for rank in range(1, amount + 1)]
    largest = most if full else min(most, max(-(-total // amount), total * weights[0] // sum(weights)))
    least = 1 if total - largest >= amount - 1 else 0
    counts, spare = [largest] + [least] * (amount - 1), total - largest - least * (amount - 1)
    while spare > 0:
        free = [i for i in range(1, amount) if counts[i] < largest] or [i for i in range(1, amount) if counts[i] < most]
        pool, remaining = sum([weights[i] for i in free]), spare
        for i in free:
            addition = min(most - counts[i], max(1, remaining * weights[i] // pool), spare)
            counts[i] = counts[i] + addition
            spare = spare - addition
    return np.array(counts)


def noise(own_key, extent, scale, most, shards=(), kind=jnp.bfloat16):
    array = scale * jax.random.normal(own_key, extent, jnp.float32)
    if shards:
        array = array * levels(own_key, extent, shards, -0.22, 0.18)
    return jnp.clip(array, -most, most).astype(kind)


def setup_inputs(seed: int = 0) -> dict:
    key_of = jax.random.split(jax.random.key(seed), 7)
    tokens = noise(key_of[0], (TOKENS, D), 1.0, 6.0, ((0, 32),))
    routes_keys = jax.random.split(jax.random.fold_in(key_of[1], 1), TOKENS // TOK_DEV)
    routes_turns = jax.random.permutation(jax.random.fold_in(key_of[1], 3), TOKENS // TOK_DEV)
    routes = jax.vmap(lambda own, number: routed_block(jax.random.fold_in(key_of[1], 2), own, number, TOK_DEV, EXPERTS, TOP, CAP, 2))(routes_keys, routes_turns).reshape((TOKENS, TOP))
    gates = jnp.clip(0.1 + 0.9 * jax.random.uniform(key_of[2], (TOKENS, TOP), jnp.float32) ** levels(key_of[2], (TOKENS, TOP), ((0, 32),), -0.2, 0.2), 0.1, 1.0)
    d_out = noise(key_of[3], (TOKENS, D), 0.5, 3.0, ((0, 32),))
    w_in = noise(key_of[4], (EXPERTS, 2, FF, D), D ** -0.5, 0.09375, ((0, 2), (2, 16)))
    w_out = noise(key_of[5], (EXPERTS, FF, D), FF ** -0.5, 0.0625, ((0, 2), (1, 16)))
    return dict(tokens=tokens, routes=routes, gates=gates, d_out=d_out, w_in=w_in, w_out=w_out)


def reference(tokens, routes, gates, d_out, w_in, w_out):
    sources = N_DP * N_EXPERT * N_TENSOR
    per_block = TOK_DEV * TOP
    route_count = TOKENS * TOP
    buffer_rows = sources * CAP
    flat_routes = routes.reshape(-1).astype(jnp.int32)
    one_hot = (flat_routes[:, None] == jnp.arange(EXPERTS, dtype=jnp.int32)[None, :]).astype(jnp.int32)
    one_hot = one_hot.reshape(sources, per_block, EXPERTS)
    earlier = jnp.cumsum(one_hot, axis=1) - one_hot
    slot_index = jnp.sum(earlier * one_hot, axis=2).reshape(-1)
    source_block = jnp.arange(route_count, dtype=jnp.int32) // per_block
    position = (source_block * CAP + slot_index).astype(jnp.int32)
    slot_table = jnp.full((EXPERTS, buffer_rows), route_count, jnp.int32)
    slot_table = slot_table.at[flat_routes, position].set(jnp.arange(route_count, dtype=jnp.int32))
    token_rows = jnp.concatenate([jnp.repeat(tokens, TOP, axis=0), jnp.zeros((1, D), jnp.bfloat16)], axis=0)
    weighted = (gates.reshape(-1, 1) * jnp.repeat(d_out, TOP, axis=0).astype(jnp.float32)).astype(jnp.bfloat16)
    weighted = jnp.concatenate([weighted, jnp.zeros((1, D), jnp.bfloat16)], axis=0)

    def expert(operands):
        table_row, weight_in, weight_out = operands
        rows_x = token_rows[table_row]
        rows_g = weighted[table_row]
        gate_pre = jnp.dot(rows_x, weight_in[0].T, preferred_element_type=jnp.float32)
        up_pre = jnp.dot(rows_x, weight_in[1].T, preferred_element_type=jnp.float32)
        sigma = jax.nn.sigmoid(gate_pre)
        hidden = (gate_pre * sigma * up_pre).astype(jnp.bfloat16)
        expert_out = jnp.dot(hidden, weight_out, preferred_element_type=jnp.float32).astype(jnp.bfloat16)
        d_hidden = jnp.dot(rows_g, weight_out.T, preferred_element_type=jnp.float32)
        d_gate = d_hidden * up_pre * sigma * (1.0 + gate_pre * (1.0 - sigma))
        d_up = d_hidden * gate_pre * sigma
        d_pre = jnp.stack([d_gate, d_up], axis=0).astype(jnp.bfloat16)
        expert_dx = (jnp.dot(d_pre[0], weight_in[0], preferred_element_type=jnp.float32)
                     + jnp.dot(d_pre[1], weight_in[1], preferred_element_type=jnp.float32)).astype(jnp.bfloat16)
        grad_down = jnp.dot(hidden.T, rows_g, preferred_element_type=jnp.float32).astype(jnp.bfloat16)
        grad_up = jnp.einsum('krf,rd->kfd', d_pre.astype(jnp.float32), rows_x.astype(jnp.float32),
                             precision=lax.Precision.HIGHEST).astype(jnp.bfloat16)
        return expert_out, expert_dx, grad_up, grad_down

    outs_all, dx_all, grad_in, grad_out = lax.map(expert, (slot_table, w_in, w_out))
    out_route = outs_all[flat_routes, position].astype(jnp.float32).reshape(TOKENS, TOP, D)
    dx_route = dx_all[flat_routes, position].astype(jnp.float32).reshape(TOKENS, TOP, D)
    mixed = jnp.sum(gates[:, :, None] * out_route, axis=1).astype(jnp.bfloat16)
    d_tokens = jnp.sum(dx_route, axis=1).astype(jnp.bfloat16)
    d_gates = jnp.sum(d_out.astype(jnp.float32)[:, None, :] * out_route, axis=2)
    return mixed, d_tokens, d_gates, grad_in, grad_out
```

```python
import jax
import jax.numpy as jnp
from jax import lax
from jax.sharding import PartitionSpec as P

ALL = ("dp", "expert", "tensor")


def dot(a, b, dims):
    return lax.dot_general(a, b, (dims, ((), ())), preferred_element_type=jnp.float32)


def split3(v):
    top = lax.reduce_precision(v, 8, 7)
    mid = lax.reduce_precision(v - top, 8, 7)
    return [top, mid, v - top - mid]


def spread(v, axis):
    copies = jnp.broadcast_to(v[None], (lax.axis_size(axis),) + v.shape)
    return lax.all_to_all(copies, axis, split_axis=0, concat_axis=0, tiled=True)


def per_device(tokens, routes, gates, d_out, w_in, w_out):
    tok_count, width = tokens.shape
    top_k = routes.shape[1]
    local_experts, _, ff, _ = w_in.shape
    n = lax.axis_size(ALL)
    first = lax.axis_index("expert") * local_experts
    small = jnp.concatenate([routes.astype(jnp.float32)] + split3(gates), axis=1)
    small = jnp.pad(small, ((0, 0), (0, 128 - small.shape[1]))).astype(jnp.bfloat16)
    sent = jnp.concatenate([tokens, d_out, small], axis=1)
    for axis in ALL:
        sent = spread(sent, axis)
    sent = sent.reshape(n * tok_count, -1)
    x = sent[:, :width]
    g = sent[:, width : 2 * width]
    extra = sent[:, 2 * width :].astype(jnp.float32)
    routes_all = extra[:, :top_k].astype(jnp.int32)
    gates_all = (
        extra[:, top_k : 2 * top_k] + extra[:, 2 * top_k : 3 * top_k] + extra[:, 3 * top_k : 4 * top_k]
    )
    names = first + jnp.arange(local_experts, dtype=jnp.int32)
    hit = (routes_all[:, :, None] == names[None, None, :]).astype(jnp.float32)
    gate = jnp.sum(gates_all[:, :, None] * hit, axis=1)
    rows = n * tok_count
    w_both = w_in.reshape(local_experts * 2 * ff, width)
    w_down = w_out.reshape(local_experts * ff, width)
    pre = dot(x, w_both, ((1,), (1,))).reshape(rows, local_experts, 2, ff)
    d_raw = dot(g, w_down, ((1,), (1,))).reshape(rows, local_experts, ff)
    gate_pre = pre[:, :, 0]
    up_pre = pre[:, :, 1]
    sigma = jax.nn.sigmoid(gate_pre)
    hidden = lax.reduce_precision(gate_pre * sigma * up_pre, 8, 7)
    scale = gate[:, :, None]
    scaled = (scale * hidden).astype(jnp.bfloat16).reshape(rows, local_experts * ff)
    dg = jnp.sum(hidden * d_raw, axis=2)
    dg_part = jnp.sum(dg[:, None, :] * hit, axis=2)
    d_hidden = scale * d_raw
    d_gate = d_hidden * up_pre * sigma * (1.0 + gate_pre * (1.0 - sigma))
    d_up = d_hidden * gate_pre * sigma
    d_pre = jnp.stack([d_gate, d_up], axis=2).astype(jnp.bfloat16).reshape(rows, -1)
    mixed_part = dot(scaled, w_down, ((1,), (0,)))
    dx_part = dot(d_pre, w_both, ((1,), (0,)))
    grad_out = dot(scaled, g, ((0,), (0,))).astype(jnp.bfloat16)
    grad_in = dot(d_pre, x, ((0,), (0,))).astype(jnp.bfloat16)
    pad = jnp.zeros((rows, 128 - 2 * top_k), jnp.bfloat16)
    sums = (mixed_part, dx_part, dg_part)
    for axis in ALL[::-1]:
        count = lax.axis_size(axis)
        mixed, d_tokens, d_gates = sums
        dg_top = lax.reduce_precision(d_gates, 8, 7)
        part = jnp.concatenate(
            [v.astype(jnp.bfloat16) for v in (mixed, d_tokens, dg_top, d_gates - dg_top)]
            + [pad[: d_gates.shape[0]]],
            axis=1,
        )
        part = part.reshape(count, -1, part.shape[1])
        got = lax.all_to_all(part, axis, split_axis=0, concat_axis=0, tiled=True)
        got = jnp.sum(got.astype(jnp.float32), axis=0)
        end = 2 * width
        d_gates = got[:, end : end + top_k] + got[:, end + top_k : end + 2 * top_k]
        sums = (got[:, :width], got[:, width:end], d_gates)
    mixed, d_tokens, d_gates = sums
    return (
        mixed.astype(jnp.bfloat16),
        d_tokens.astype(jnp.bfloat16),
        d_gates,
        grad_in.reshape(w_in.shape),
        grad_out.reshape(w_out.shape),
    )


def solution(mesh):
    return jax.shard_map(
        per_device,
        mesh=mesh,
        in_specs=(
            P(("dp", "expert", "tensor"), None),
            P(("dp", "expert", "tensor"), None),
            P(("dp", "expert", "tensor"), None),
            P(("dp", "expert", "tensor"), None),
            P("expert", None, ("dp", "tensor"), None),
            P("expert", ("dp", "tensor"), None),
        ),
        out_specs=(
            P(("dp", "expert", "tensor"), None),
            P(("dp", "expert", "tensor"), None),
            P(("dp", "expert", "tensor"), None),
            P("expert", None, ("dp", "tensor"), None),
            P("expert", ("dp", "tensor"), None),
        ),
        check_vma=False,
    )
```
